256 devices in a mesh: row: 16 (over y, x), col: 16 (over z, core).
Axes of the slice: x: 4, y: 4, z: 8, core: 2. Of those that a mesh axis runs over, the one named last changes fastest.
Arguments:
- g0_values: bfloat16 [8192, 8192], P('row', 'col'), may hold values from -6 to 6
- g0_pattern: int32 [64, 64], P('row', 'col'), may hold values 0 or 1
- sigma_values: bfloat16 [16, 96, 128, 128], P('row', 'col'), may hold values from -0.0014648438 to 0.0014648438
- sigma_pairs: int32 [16, 96, 2], P('row', 'col'), may hold values from 0 to 63, as said below
- sigma_count: int32 [16, 16], P('row', 'col'), may hold values from 1 to 6, as said below
Outputs:
- g_full: bfloat16 [8192, 8192], P('row', 'col')
The draws below stay inside these ranges and needn't reach their ends.
Inputs may be any that keep to these rules, and one draw needn't show every extreme that they name: `sigma_pairs`: slot pairs of the device at position (g, o) name blocks with block row in g * 4 to g * 4 + 3 and block column in o * 4 to o * 4 + 3; the pairs of one device are distinct. `sigma_count`: count of live slots, which are the first ones of a device.
All inputs are finite; a program needn't handle non-finite values. No bound on the sum of `g0_pattern` on one device may be relied on, other than what follows from the above.
Results may differ from the reference program's by a relative error of at most 0.0037.
Values may be sent and summed in bfloat16 or wider, within the bound.
A program may use at most 128 MiB of HBM per device.

```python
import jax
import jax.numpy as jnp

B = 128
CB = 4
GROUPS = 16
OWNERS = 16
NB = 64
RB = 4
SLOTS = 6


def draw_sigma_pairs(key, part):
    places = RB * CB
    scores = jax.random.randint(key, (GROUPS, OWNERS, places), 0, 1 << 20) * places + jnp.arange(places, dtype=jnp.int32)
    order = jnp.argsort(scores, axis=-1)[:, :, :SLOTS].astype(jnp.int32)
    rows_k = jnp.arange(GROUPS, dtype=jnp.int32)[:, None, None] * RB + order // CB
    cols_j = jnp.arange(OWNERS, dtype=jnp.int32)[None, :, None] * CB + order % CB
    pairs = jnp.stack([rows_k, cols_j], axis=-1)
    return pairs.reshape(GROUPS, OWNERS * SLOTS, 2).astype(jnp.int32)


def draw_sigma_count(key, part):
    total = GROUPS * OWNERS
    counts = jax.random.randint(key, (total,), 1, SLOTS + 1)
    chosen = jax.random.randint(jax.random.fold_in(key, 7), (), 0, total)
    counts = counts.at[chosen].set(SLOTS)
    counts = counts.at[(chosen + 1) % total].set(1)
    return counts.reshape(GROUPS, OWNERS).astype(jnp.int32)


def set_ends(array, stream_key, low, top_value):
    index_at = [jax.random.randint(jax.random.fold_in(stream_key, axis), (), 0, length) for axis, length in enumerate(array.shape)]
    main_axis = array.shape.index(max(array.shape))
    next_to = index_at[:main_axis] + [(index_at[main_axis] + 1) % array.shape[main_axis]] + index_at[main_axis + 1:]
    return array.at[tuple(index_at)].set(low).at[tuple(next_to)].set(top_value)


def block_levels(key, extent, pieces, smallest, top_value):
    factor_of, own = 1.0, jax.random.fold_in(key, 6)
    for position, blocks in pieces:
        steps = jnp.exp(jax.random.uniform(jax.random.fold_in(own, position), (blocks,), jnp.float32, smallest / len(pieces), top_value / len(pieces)))
        factor_of = factor_of * jnp.repeat(steps, extent[position] // blocks).reshape([-1 if axis == position else 1 for axis in range(len(extent))])
    return factor_of


def gaussian(stream_key, shape, deviation, reach, split=(), held_as=jnp.bfloat16):
    result = jax.random.normal(stream_key, shape, jnp.float32) * deviation
    if len(split) > 0:
        result = block_levels(stream_key, shape, split, -0.22, 0.18) * result
    return jnp.clip(result, min=-reach, max=reach).astype(held_as)


def setup_inputs(seed: int = 0) -> dict:
    arg_keys = jax.random.split(jax.random.key(seed), 6)
    return {
        "g0_values": gaussian(arg_keys[0], (NB * B, NB * B), 1.0, 6.0, ((0, 16), (1, 16))),
        "g0_pattern": set_ends((jax.random.randint(arg_keys[1], (NB, NB), 0, 4) < 3).astype(jnp.int32), jax.random.fold_in(arg_keys[1], 1), 0, 1),
        "sigma_values": gaussian(arg_keys[2], (GROUPS, OWNERS * SLOTS, B, B), (2.0 / (NB * B)), 0.0014648438, ((0, 16), (1, 16))),
        "sigma_pairs": draw_sigma_pairs(jax.random.fold_in(arg_keys[5], 71), 0),
        "sigma_count": draw_sigma_count(jax.random.fold_in(arg_keys[5], 71), 0),
    }


def reference(g0_values, g0_pattern, sigma_values, sigma_pairs, sigma_count):
    mask = jnp.repeat(jnp.repeat(g0_pattern, B, axis=0), B, axis=1)
    g0 = g0_values * mask.astype(jnp.bfloat16)
    slot_index = jnp.arange(OWNERS * SLOTS, dtype=jnp.int32)
    owner_index = slot_index // SLOTS
    live = (slot_index % SLOTS)[None, :] < sigma_count[:, owner_index]
    rows_k = jnp.where(live, sigma_pairs[:, :, 0], NB).reshape(-1).astype(jnp.int32)
    cols_j = (sigma_pairs[:, :, 1]).reshape(-1).astype(jnp.int32)
    blocks = sigma_values.reshape(-1, B, B)
    dense = jnp.zeros((NB, B, NB, B), jnp.bfloat16)
    dense = dense.at[rows_k, :, cols_j, :].add(blocks, mode="drop")
    sigma = dense.reshape(NB * B, NB * B)
    left = jnp.dot(g0, sigma, preferred_element_type=jnp.float32).astype(jnp.bfloat16)
    total = g0.astype(jnp.float32) + jnp.dot(left, g0, preferred_element_type=jnp.float32)
    return total.astype(jnp.bfloat16)
```

```python
import functools
import heapq

import jax
import jax.numpy as jnp
from jax import lax
from jax.experimental import pallas as pl
from jax.experimental.pallas import tpu as pltpu
from jax.sharding import PartitionSpec as P

MESH = pl.DeviceIdType.MESH
NX, NY, NZ = 4, 4, 8
ROWS = NX * NY
COLS = NZ * 2
CH = 2
SLOT_ROWS = 832

LINK = 47.0e3
CORE = 400.0e3
HOP = 1.5


def kernel(
    g0_ref, sig_ref, pat_ref, pairs_ref, count_ref, out_ref,
    gr, gc, lr, sc, sd, lacc, cacc, send_sems, recv_sems,
):
    tile = g0_ref.shape[0]
    width = sig_ref.shape[1]
    nblk = tile // width
    slots = sig_ref.shape[0] // width
    ch_rows = tile // CH
    row = lax.axis_index("row")
    col = lax.axis_index("col")
    x, y = lax.rem(row, NX), row // NX
    z, c = col // 2, lax.rem(col, 2)

    def wrap(v, n):
        return lax.rem(v + n, n)

    def device(dx=0, dy=0, dz=0, dc=0):
        xx, yy, zz = wrap(x + dx, NX), wrap(y + dy, NY), wrap(z + dz, NZ)
        cc = 1 - c if dc else c
        return (yy * NX + xx, zz * 2 + cc)

    barrier = pltpu.get_barrier_semaphore()
    near = [device(dx=1), device(dx=-1), device(dy=1), device(dy=-1), device(dz=1), device(dz=-1), device(dc=1)]
    for d in near:
        pl.semaphore_signal(barrier, inc=1, device_id=d, device_id_type=MESH)

    for a in range(nblk):
        for b in range(nblk):
            ra, rb = pl.ds(a * width, width), pl.ds(b * width, width)
            block = g0_ref[ra, rb]
            block = jnp.where(pat_ref[a, b] != 0, block, jnp.zeros_like(block))
            gc[row, ra, rb] = block
            h, off = divmod(a * width, ch_rows)
            gr[h, col, pl.ds(off, width), rb] = block
            cacc[h, pl.ds(off, width), rb] = block.astype(jnp.float32)

    sc[row, pl.ds(0, slots * width), :] = sig_ref[...]
    place = lax.broadcasted_iota(jnp.int32, (nblk * nblk, width), 0)
    table = jnp.full((nblk * nblk, width), -1.0, jnp.float32)
    for s in range(slots):
        at = lax.rem(pairs_ref[s, 0], nblk) * nblk + lax.rem(pairs_ref[s, 1], nblk)
        at = jnp.where(s < count_ref[0, 0], at, -1)
        table = jnp.where(place == at, float(s), table)
    sc[row, pl.ds(slots * width, nblk * nblk), :] = table.astype(jnp.bfloat16)
    tail = slots * width + nblk * nblk
    sc[row, pl.ds(tail, SLOT_ROWS - tail), :] = jnp.zeros((SLOT_ROWS - tail, width), jnp.bfloat16)

    pl.semaphore_wait(barrier, len(near))

    waits = {}
    sends = []
    state = {"now": 0.0, "seq": 0, "done": set()}
    link_free = {}
    heap = []
    actions = {}
    pending = []
    ids = {}

    def push(time, kind, name):
        state["seq"] += 1
        heapq.heappush(heap, (time, kind, state["seq"], name))

    def send(name, src, dst, link, dev, nbytes, landed, after):
        i = ids.setdefault(name, len(ids))
        copy = pltpu.make_async_remote_copy(
            src_ref=src, dst_ref=dst, send_sem=send_sems.at[i], recv_sem=recv_sems.at[i],
            device_id=dev, device_id_type=MESH,
        )
        copy.start()
        sends.append(copy)
        rate = CORE if link == "c" else LINK
        t = max(state["now"], link_free.get(link, 0.0)) + nbytes / rate
        link_free[link] = t

        def act():
            pltpu.make_async_remote_copy(
                src_ref=landed, dst_ref=landed, send_sem=send_sems.at[i], recv_sem=recv_sems.at[i],
                device_id=dev, device_id_type=MESH,
            ).wait_recv()
            if after is not None:
                after()

        actions[name] = (act, 0.05)
        push(t + HOP, 0, name)

    def step(name, needs, fn, cost):
        actions[name] = (fn, cost)
        pending.append((set(needs), name))

    def settle():
        for item in list(pending):
            if item[0] <= state["done"]:
                pending.remove(item)
                push(state["now"], 1, item[1])

    def run():
        settle()
        while heap:
            ready = [e for e in heap if e[0] <= state["now"]]
            e = min(ready, key=lambda e: (e[1], e[0], e[2])) if ready else heap[0]
            heap.remove(e)
            heapq.heapify(heap)
            fn, cost = actions[e[3]]
            state["now"] = max(state["now"], e[0]) + cost
            fn()
            state["done"].add(e[3])
            settle()
        assert not pending, pending

    def z_stream(tag, buf, h):
        half = ch_rows // 2
        nbytes = ch_rows * tile * 2

        def piece(zz, cc, part):
            r = buf.at[h, wrap(zz, NZ) * 2 + cc]
            return r if part is None else r.at[pl.ds(part * half, half), :]

        def to_core(name, zz, part):
            src = piece(zz, c, part)
            n = nbytes if part is None else nbytes // 2
            send(name, src, src, "c", device(dc=1), n, piece(zz, 1 - c, part), None)

        def hop(direction, k):
            part = None if k < NZ // 2 else (0 if direction > 0 else 1)
            src = piece(z - direction * (k - 1), c, part)
            n = nbytes if part is None else nbytes // 2

            def after():
                if k < NZ // 2:
                    hop(direction, k + 1)
                to_core((tag, "c", h, direction, k), z - direction * k, part)

            send((tag, "z", h, direction, k), src, src, ("z", direction), device(dz=direction), n,
                 piece(z - direction * k, c, part), after)

        hop(1, 1)
        hop(-1, 1)
        to_core((tag, "c", h, 0, 0), z, None)

    def z_needs(tag, h, k):
        if k == 0:
            return [(tag, "c", h, 0, 0)]
        return [(tag, s, h, d, k) for s in ("z", "c") for d in (1, -1)]

    def xy_stream(tag, buf, rows, nbytes):
        q = rows // 4
        names = []

        def piece(dx, dy, half, part):
            r = buf.at[wrap(y + dy, NY) * NX + wrap(x + dx, NX)]
            if part is None:
                return r.at[pl.ds(half * 2 * q, 2 * q), :]
            return r.at[pl.ds((half * 2 + part) * q, q), :]

        def off(half, first, second):
            return (first, second) if half == 0 else (second, first)

        def second_phase(half, at):
            axis = "y" if half == 0 else "x"

            def hop(direction, k):
                part = None if k == 1 else (0 if direction > 0 else 1)
                src = piece(*off(half, at, -direction * (k - 1)), half, part)
                land = piece(*off(half, at, -direction * k), half, part)
                n = nbytes // 2 if k == 1 else nbytes // 4
                name = (tag, half, 2, at, direction, k)
                names.append(name)
                send(name, src, src, (axis, direction), device(**{"d" + axis: direction}), n, land,
                     (lambda: hop(direction, 2)) if k == 1 else None)

            hop(1, 1)
            hop(-1, 1)

        def first_phase(half):
            axis = "x" if half == 0 else "y"
            far = []

            def hop(direction, k):
                part = None if k == 1 else (0 if direction > 0 else 1)
                src = piece(*off(half, -direction * (k - 1), 0), half, part)
                land = piece(*off(half, -direction * k, 0), half, part)
                n = nbytes // 2 if k == 1 else nbytes // 4
                name = (tag, half, 1, direction, k)
                names.append(name)

                def after():
                    if k == 1:
                        hop(direction, 2)
                        second_phase(half, -direction)
                    else:
                        far.append(direction)
                        if len(far) == 2:
                            second_phase(half, 2)

                send(name, src, src, (axis, direction), device(**{"d" + axis: direction}), n, land, after)

            hop(1, 1)
            hop(-1, 1)

        for half in (0, 1):
            first_phase(half)
        for half in (0, 1):
            second_phase(half, 0)
        return 80 // 2

    def xy_all(tag):
        need = []
        for half in (0, 1):
            for d in (1, -1):
                for k in (1, 2):
                    need.append((tag, half, 1, d, k))
                    need.extend((tag, half, 2, at, d, k) for at in (0, 1, -1, 2))
        return need

    def expand(first, n):
        @pl.loop(first, first + n)
        def _(r):
            t = sc[r, pl.ds(slots * width, nblk * nblk), :].astype(jnp.float32)
            for b in range(nblk * nblk):
                line = t[b : b + 1, :]
                total = jnp.zeros((width, width), jnp.bfloat16)
                for s in range(slots):
                    on = jnp.where(line == float(s), 1.0, 0.0).astype(jnp.bfloat16)
                    total = total + sc[r, pl.ds(s * width, width), :] * on
                sd[r, pl.ds((b // nblk) * width, width), pl.ds((b % nblk) * width, width)] = total

    def dots(acc, left_buf, right_buf, h, k):
        far = NZ // 2
        n = 2 if k in (0, far) else 4

        @pl.loop(0, n)
        def _(i):
            cc = lax.rem(i, 2)
            sign = 1 - 2 * (i // 2)
            t = wrap(z + sign * k, NZ) * 2 + cc
            acc[h] += jnp.dot(left_buf[h, t], right_buf[t], preferred_element_type=jnp.float32)

    def finish_left(h):
        lr[h, col] = lacc[h].astype(jnp.bfloat16)
        z_stream("L", lr, h)

    def finish(h):
        out_ref[pl.ds(h * ch_rows, ch_rows), :] = cacc[h].astype(jnp.bfloat16)

    lacc[...] = jnp.zeros_like(lacc)
    xy_stream("S", sc, SLOT_ROWS, SLOT_ROWS * width * 2)
    for h in range(CH):
        z_stream("G", gr, h)
    xy_stream("C", gc, tile, tile * tile * 2)

    group = 4
    for i in range(ROWS // group):
        step(("expand", i), xy_all("S") + ([("expand", i - 1)] if i else []), functools.partial(expand, i * group, group), 1.0)
    last = ("expand", ROWS // group - 1)
    far = NZ // 2
    for h in range(CH):
        for k in range(far + 1):
            step(("left", h, k), z_needs("G", h, k) + [last], functools.partial(dots, lacc, gr, sd, h, k), 1.0)
            step(("prod", h, k), z_needs("L", h, k) + xy_all("C") + [("left done", h)],
                 functools.partial(dots, cacc, lr, gc, h, k), 1.0)
        step(("left done", h), [("left", h, k) for k in range(far + 1)], functools.partial(finish_left, h), 0.3)
        step(("done", h), [("prod", h, k) for k in range(far + 1)], functools.partial(finish, h), 0.3)
    run()
    for copy in sends:
        copy.wait_send()
    assert len(ids) == N_COPIES, len(ids)


N_COPIES = 2 * 40 + 2 * CH * (2 * (NZ // 2) * 2 + 1)


def per_device(g0_values, g0_pattern, sigma_values, sigma_pairs, sigma_count):
    tile = g0_values.shape[0]
    _, slots, width, _ = sigma_values.shape
    bf, f32 = jnp.bfloat16, jnp.float32
    vmem = pl.BlockSpec(memory_space=pltpu.VMEM)
    smem = pl.BlockSpec(memory_space=pltpu.SMEM)
    return pl.pallas_call(
        kernel,
        name="dyson",
        out_shape=jax.ShapeDtypeStruct((tile, tile), bf),
        in_specs=[vmem, vmem, smem, smem, smem],
        out_specs=vmem,
        scratch_shapes=[
            pltpu.VMEM((CH, COLS, tile // CH, tile), bf),
            pltpu.VMEM((ROWS, tile, tile), bf),
            pltpu.VMEM((CH, COLS, tile // CH, tile), bf),
            pltpu.VMEM((ROWS, SLOT_ROWS, width), bf),
            pltpu.VMEM((ROWS, tile, tile), bf),
            pltpu.VMEM((CH, tile // CH, tile), f32),
            pltpu.VMEM((CH, tile // CH, tile), f32),
            pltpu.SemaphoreType.DMA((N_COPIES,)),
            pltpu.SemaphoreType.DMA((N_COPIES,)),
        ],
        compiler_params=pltpu.CompilerParams(
            collective_id=0, has_side_effects=True, vmem_limit_bytes=58 << 20
        ),
    )(
        g0_values,
        sigma_values.reshape(slots * width, width),
        g0_pattern,
        sigma_pairs.reshape(slots, 2),
        sigma_count,
    )


def solution(mesh):
    placed = (
        P("row", "col"),
        P("row", "col"),
        P("row", "col", None, None),
        P("row", "col", None),
        P("row", "col"),
    )
    return jax.shard_map(
        per_device, mesh=mesh, in_specs=placed, out_specs=P("row", "col"), check_vma=False
    )
```

```python
import functools
import heapq

import jax
import jax.numpy as jnp
from jax import lax
from jax.experimental import pallas as pl
from jax.experimental.pallas import tpu as pltpu
from jax.sharding import PartitionSpec as P

MESH = pl.DeviceIdType.MESH
NX, NY, NZ = 4, 4, 8
ROWS = NX * NY
COLS = NZ * 2
CH = 2
SLOT_ROWS = 832

RATE = {"x": 40.0e3, "y": 40.0e3, "z": 46.0e3, "c": 250.0e3}
HOP = 1.5
WINDOW = {"x": 2, "y": 2, "z": 99, "c": 99}


def kernel(
    g0_ref, sig_ref, pat_ref, pairs_ref, count_ref, out_ref,
    gr, gc, lr, sc, sd, lacc, cacc, send_sems, recv_sems,
):
    tile = g0_ref.shape[0]
    width = sig_ref.shape[1]
    nblk = tile // width
    slots = sig_ref.shape[0] // width
    ch_rows = tile // CH
    row = lax.axis_index("row")
    col = lax.axis_index("col")
    x, y = lax.rem(row, NX), row // NX
    z, c = col // 2, lax.rem(col, 2)

    def wrap(v, n):
        return lax.rem(v + n, n)

    def device(dx=0, dy=0, dz=0, dc=0):
        xx, yy, zz = wrap(x + dx, NX), wrap(y + dy, NY), wrap(z + dz, NZ)
        cc = 1 - c if dc else c
        return (yy * NX + xx, zz * 2 + cc)

    barrier = pltpu.get_barrier_semaphore()
    near = [device(dx=1), device(dx=-1), device(dy=1), device(dy=-1), device(dz=1), device(dz=-1), device(dc=1)]
    for d in near:
        pl.semaphore_signal(barrier, inc=1, device_id=d, device_id_type=MESH)

    for a in range(nblk):
        for b in range(nblk):
            ra, rb = pl.ds(a * width, width), pl.ds(b * width, width)
            block = g0_ref[ra, rb]
            block = jnp.where(pat_ref[a, b] != 0, block, jnp.zeros_like(block))
            gc[row, ra, rb] = block
            gr[col, ra, rb] = block
            cacc[ra, rb] = block.astype(jnp.float32)

    sc[row, pl.ds(0, slots * width), :] = sig_ref[...]
    place = lax.broadcasted_iota(jnp.int32, (nblk * nblk, width), 0)
    table = jnp.full((nblk * nblk, width), -1.0, jnp.float32)
    for s in range(slots):
        at = lax.rem(pairs_ref[0, s], nblk) * nblk + lax.rem(pairs_ref[1, s], nblk)
        at = jnp.where(s < count_ref[0, 0], at, -1)
        table = jnp.where(place == at, float(s), table)
    sc[row, pl.ds(slots * width, nblk * nblk), :] = table.astype(jnp.bfloat16)
    tail = slots * width + nblk * nblk
    sc[row, pl.ds(tail, SLOT_ROWS - tail), :] = jnp.zeros((SLOT_ROWS - tail, width), jnp.bfloat16)

    pl.semaphore_wait(barrier, len(near))

    sends = []
    state = {"now": 0.0, "seq": 0, "done": set()}
    link_free, queues, flying = {}, {}, {}
    heap = []
    actions = {}
    pending = []
    ids = {}

    def push(time, kind, name):
        state["seq"] += 1
        heapq.heappush(heap, (time, kind, state["seq"], name))

    def start(link):
        while queues[link] and flying[link] < WINDOW[link[0]]:
            urgent = [e for e in queues[link] if e[0][0] == "S"]
            entry = urgent[0] if urgent else queues[link][0]
            queues[link].remove(entry)
            name, src, dst, dev, nbytes, landed, after = entry
            flying[link] += 1
            i = ids.setdefault(name, len(ids))
            copy = pltpu.make_async_remote_copy(
                src_ref=src, dst_ref=dst, send_sem=send_sems.at[i], recv_sem=recv_sems.at[i],
                device_id=dev, device_id_type=MESH,
            )
            copy.start()
            sends.append(copy)
            rate = RATE[link[0]]
            t = max(state["now"], link_free.get(link, 0.0)) + nbytes / rate
            link_free[link] = t
            actions[name] = (functools.partial(arrive, link, i, landed, dev, after), 0.1)
            push(t + HOP, 0, name)

    def arrive(link, i, landed, dev, after):
        pltpu.make_async_remote_copy(
            src_ref=landed, dst_ref=landed, send_sem=send_sems.at[i], recv_sem=recv_sems.at[i],
            device_id=dev, device_id_type=MESH,
        ).wait_recv()
        flying[link] -= 1
        if after is not None:
            after()
        start(link)

    def send(name, src, dst, link, dev, nbytes, landed, after):
        queues.setdefault(link, []).append((name, src, dst, dev, nbytes, landed, after))
        flying.setdefault(link, 0)
        start(link)

    def step(name, needs, fn, cost):
        actions[name] = (fn, cost)
        pending.append((set(needs), name))

    def settle():
        for item in list(pending):
            if item[0] <= state["done"]:
                pending.remove(item)
                push(state["now"], 1, item[1])

    def run():
        settle()
        while heap:
            ready = [e for e in heap if e[0] <= state["now"]]
            e = min(ready, key=lambda e: (e[1], e[0], e[2])) if ready else heap[0]
            heap.remove(e)
            heapq.heapify(heap)
            fn, cost = actions[e[3]]
            state["now"] = max(state["now"], e[0]) + cost
            fn()
            state["done"].add(e[3])
            settle()
        assert not pending, pending

    def z_stream(tag, buf, h):
        half = ch_rows // 2
        nbytes = ch_rows * tile * 2

        def piece(zz, cc, part):
            r = buf.at[wrap(zz, NZ) * 2 + cc]
            if part is None:
                return r.at[pl.ds(h * ch_rows, ch_rows), :]
            return r.at[pl.ds(h * ch_rows + part * half, half), :]

        def to_core(name, zz, part):
            src = piece(zz, c, part)
            n = nbytes if part is None else nbytes // 2
            send(name, src, src, ("c", 0), device(dc=1), n, piece(zz, 1 - c, part), None)

        def hop(direction, k):
            part = None if k < NZ // 2 else (0 if direction > 0 else 1)
            src = piece(z - direction * (k - 1), c, part)
            n = nbytes if part is None else nbytes // 2

            def after():
                if k < NZ // 2:
                    hop(direction, k + 1)
                to_core((tag, "c", h, direction, k), z - direction * k, part)

            send((tag, "z", h, direction, k), src, src, ("z", direction), device(dz=direction), n,
                 piece(z - direction * k, c, part), after)

        hop(1, 1)
        hop(-1, 1)
        to_core((tag, "c", h, 0, 0), z, None)

    def z_needs(tag, h, k):
        if k == 0:
            return [(tag, "c", h, 0, 0)]
        return [(tag, s, h, d, k) for s in ("z", "c") for d in (1, -1)]

    def xy_stream(tag, buf, rows, nbytes):
        q = rows // 4

        def piece(dx, dy, half, part):
            r = buf.at[wrap(y + dy, NY) * NX + wrap(x + dx, NX)]
            if part is None:
                return r.at[pl.ds(half * 2 * q, 2 * q), :]
            return r.at[pl.ds((half * 2 + part) * q, q), :]

        def off(half, first, second):
            return (first, second) if half == 0 else (second, first)

        def second_phase(half, at):
            axis = "y" if half == 0 else "x"

            def hop(direction, k):
                part = None if k == 1 else (0 if direction > 0 else 1)
                src = piece(*off(half, at, -direction * (k - 1)), half, part)
                land = piece(*off(half, at, -direction * k), half, part)
                n = nbytes // 2 if k == 1 else nbytes // 4
                name = (tag, half, 2, at, direction, k)
                send(name, src, src, (axis, direction), device(**{"d" + axis: direction}), n, land,
                     (lambda: hop(direction, 2)) if k == 1 else None)

            hop(1, 1)
            hop(-1, 1)

        def first_phase(half):
            axis = "x" if half == 0 else "y"
            far = []

            def hop(direction, k):
                part = None if k == 1 else (0 if direction > 0 else 1)
                src = piece(*off(half, -direction * (k - 1), 0), half, part)
                land = piece(*off(half, -direction * k, 0), half, part)
                n = nbytes // 2 if k == 1 else nbytes // 4
                name = (tag, half, 1, direction, k)

                def after():
                    if k == 1:
                        hop(direction, 2)
                        second_phase(half, -direction)
                    else:
                        far.append(direction)
                        if len(far) == 2:
                            second_phase(half, 2)

                send(name, src, src, (axis, direction), device(**{"d" + axis: direction}), n, land, after)

            hop(1, 1)
            hop(-1, 1)

        for half in (0, 1):
            first_phase(half)
        for half in (0, 1):
            second_phase(half, 0)

    def xy_needs(tag, dx, dy):
        need = []
        for half, (first, second) in enumerate(((dx, dy), (dy, dx))):
            if second == 0:
                need.extend((tag, half, 1, d, abs(first)) for d in ((1, -1) if first == 2 else (-first,)) if first)
            else:
                need.extend((tag, half, 2, first, d, abs(second)) for d in ((1, -1) if second == 2 else (-second,)))
        return need

    def xy_all(tag):
        steps = (0, 1, -1, 2)
        return [n for dx in steps for dy in steps for n in xy_needs(tag, dx, dy)]

    def expand(dxs, dys):
        strip = width // 2

        @pl.loop(0, len(dxs) * len(dys))
        def _(i):
            dx = dxs[0] + (i // len(dys)) * dxs.step
            dy = dys[0] + lax.rem(i, len(dys)) * dys.step
            r = wrap(y + dy, NY) * NX + wrap(x + dx, NX)
            t = sc[r, pl.ds(slots * width, nblk * nblk), :].astype(jnp.float32)
            for u in range(width // strip):
                held = [sc[r, pl.ds(s * width + u * strip, strip), :].reshape(strip // 16, 16, width) for s in range(slots)]
                for b in range(nblk * nblk):
                    line = jnp.broadcast_to(t[b : b + 1, :], (16, width))
                    total = None
                    for s in range(slots):
                        on = jnp.where(line == float(s), 1.0, 0.0).astype(jnp.bfloat16)
                        term = held[s] * on[None]
                        total = term if total is None else total + term
                    at = (b // nblk) * width + u * strip
                    sd[r, pl.ds(at, strip), pl.ds((b % nblk) * width, width)] = total.reshape(strip, width)

    def dots(acc, left_buf, right_buf, k, first, rows):
        n = 2 if k in (0, NZ // 2) else 4
        span = pl.ds(first, rows)

        @pl.loop(0, n)
        def _(i):
            cc = lax.rem(i, 2)
            sign = 1 - 2 * (i // 2)
            t = wrap(z + sign * k, NZ) * 2 + cc
            acc[span, :] += jnp.dot(left_buf[t, span, :], right_buf[t], preferred_element_type=jnp.float32)

    def finish_left(h):
        span = pl.ds(h * ch_rows, ch_rows)
        lr[col, span, :] = lacc[span, :].astype(jnp.bfloat16)
        z_stream("L", lr, h)

    def finish(h):
        span = pl.ds(h * ch_rows, ch_rows)
        out_ref[span, :] = cacc[span, :].astype(jnp.bfloat16)

    lacc[...] = jnp.zeros_like(lacc)
    xy_stream("S", sc, SLOT_ROWS, SLOT_ROWS * width * 2)
    for h in range(CH):
        z_stream("G", gr, h)
    xy_stream("C", gc, tile, tile * tile * 2)

    zero, near1, pair, two = range(0, 1), range(-1, 2), range(-1, 2, 2), range(2, 3)
    shapes = ((near1, zero), (zero, pair), (pair, pair), (two, range(-1, 3)), (near1, two))
    for i, (dxs, dys) in enumerate(shapes):
        needs = [n for dx in dxs for dy in dys for n in xy_needs("S", dx, dy)]
        step(("expand", i), needs, functools.partial(expand, dxs, dys), 0.3 * len(dxs) * len(dys))
    dense = [("expand", i) for i in range(len(shapes))]
    both = range(CH)
    far = NZ // 2
    for k in range(far):
        needs = [n for h in both for n in z_needs("G", h, k)]
        step(("left", k), needs + dense, functools.partial(dots, lacc, gr, sd, k, 0, tile), 1.6)
        needs = [n for h in both for n in z_needs("L", h, k)] + [("left done", h) for h in both]
        step(("prod", k), needs + xy_all("C"), functools.partial(dots, cacc, lr, gc, k, 0, tile), 1.6)
    for h in both:
        step(("left last", h), z_needs("G", h, far) + dense + [("left", k) for k in range(far)],
             functools.partial(dots, lacc, gr, sd, far, h * ch_rows, ch_rows), 0.6)
        step(("left done", h), [("left last", h)], functools.partial(finish_left, h), 0.3)
        step(("prod last", h), z_needs("L", h, far) + [("prod", k) for k in range(far)],
             functools.partial(dots, cacc, lr, gc, far, h * ch_rows, ch_rows), 0.6)
        step(("done", h), [("prod last", h)], functools.partial(finish, h), 0.3)
    run()
    for copy in sends:
        copy.wait_send()
    assert len(ids) == N_COPIES, len(ids)


N_COPIES = 2 * 40 + 2 * CH * (2 * (NZ // 2) * 2 + 1)


def per_device(g0_values, g0_pattern, sigma_values, sigma_pairs, sigma_count):
    tile = g0_values.shape[0]
    _, slots, width, _ = sigma_values.shape
    bf, f32 = jnp.bfloat16, jnp.float32
    vmem = pl.BlockSpec(memory_space=pltpu.VMEM)
    smem = pl.BlockSpec(memory_space=pltpu.SMEM)
    return pl.pallas_call(
        kernel,
        name="dyson",
        out_shape=jax.ShapeDtypeStruct((tile, tile), bf),
        in_specs=[vmem, vmem, smem, smem, smem],
        out_specs=vmem,
        scratch_shapes=[
            pltpu.VMEM((COLS, tile, tile), bf),
            pltpu.VMEM((ROWS, tile, tile), bf),
            pltpu.VMEM((COLS, tile, tile), bf),
            pltpu.VMEM((ROWS, SLOT_ROWS, width), bf),
            pltpu.VMEM((ROWS, tile, tile), bf),
            pltpu.VMEM((tile, tile), f32),
            pltpu.VMEM((tile, tile), f32),
            pltpu.SemaphoreType.DMA((N_COPIES,)),
            pltpu.SemaphoreType.DMA((N_COPIES,)),
        ],
        compiler_params=pltpu.CompilerParams(
            collective_id=0, has_side_effects=True, vmem_limit_bytes=58 << 20
        ),
    )(
        g0_values,
        sigma_values.reshape(slots * width, width),
        g0_pattern,
        sigma_pairs.reshape(slots, 2).T,
        sigma_count,
    )


def solution(mesh):
    placed = (
        P("row", "col"),
        P("row", "col"),
        P("row", "col", None, None),
        P("row", "col", None),
        P("row", "col"),
    )
    return jax.shard_map(
        per_device, mesh=mesh, in_specs=placed, out_specs=P("row", "col"), check_vma=False
    )
```

```python
import functools
import heapq

import jax
import jax.numpy as jnp
from jax import lax
from jax.experimental import pallas as pl
from jax.experimental.pallas import tpu as pltpu
from jax.sharding import PartitionSpec as P

MESH = pl.DeviceIdType.MESH
NX, NY, NZ = 4, 4, 8
ROWS = NX * NY
COLS = NZ * 2
SPLIT = (192, 320)
STARTS = (0, 192)
CH = len(SPLIT)
SLOT_ROWS = 832

RATE = {"x": 40.0e3, "y": 40.0e3, "z": 46.0e3, "c": 250.0e3}
HOP = 1.5
WINDOW = {"x": 2, "y": 2, "z": 2, "c": 99}


def kernel(
    g0_ref, sig_ref, pat_hbm, pairs_hbm, count_ref, out_ref,
    pat_ref, pairs_ref, raw, gr, gc, lr, sc, sd, lacc, cacc, send_sems, recv_sems, local_sems,
):
    tile = g0_ref.shape[0]
    width = sig_ref.shape[1]
    nblk = tile // width
    slots = sig_ref.shape[0] // width
    row = lax.axis_index("row")
    col = lax.axis_index("col")
    x, y = lax.rem(row, NX), row // NX
    z, c = col // 2, lax.rem(col, 2)

    def wrap(v, n):
        return lax.rem(v + n, n)

    def device(dx=0, dy=0, dz=0, dc=0):
        xx, yy, zz = wrap(x + dx, NX), wrap(y + dy, NY), wrap(z + dz, NZ)
        cc = 1 - c if dc else c
        return (yy * NX + xx, zz * 2 + cc)

    barrier = pltpu.get_barrier_semaphore()
    near = [device(dx=1), device(dx=-1), device(dy=1), device(dy=-1), device(dz=1), device(dz=-1), device(dc=1)]
    for d in near:
        pl.semaphore_signal(barrier, inc=1, device_id=d, device_id_type=MESH)

    load_g0 = pltpu.make_async_copy(g0_ref, raw, local_sems.at[0])
    load_sig = pltpu.make_async_copy(sig_ref, sc.at[row, pl.ds(0, slots * width), :], local_sems.at[1])
    small = [
        pltpu.make_async_copy(src, dst, local_sems.at[2 + i])
        for i, (src, dst) in enumerate(((pat_hbm, pat_ref), (pairs_hbm, pairs_ref)))
    ]
    for copy in (load_g0, *small, load_sig):
        copy.start()

    def own_blocks():
        for a in range(nblk):
            for b in range(nblk):
                at = (pl.ds(a * width, width), pl.ds(b * width, width))
                block = raw[at]
                yield at, jnp.where(pat_ref[a, b] != 0, block, jnp.zeros_like(block))

    def own_table():
        place = lax.broadcasted_iota(jnp.int32, (nblk * nblk, width), 0)
        count = jnp.broadcast_to(count_ref[...], place.shape)
        table = jnp.full((nblk * nblk, width), -1.0, jnp.float32)
        for s in range(slots):
            at = lax.rem(pairs_ref[0, s], nblk) * nblk + lax.rem(pairs_ref[1, s], nblk)
            table = jnp.where((place == at) & (s < count), float(s), table)
        sc[row, pl.ds(slots * width, nblk * nblk), :] = table.astype(jnp.bfloat16)
        tail = slots * width + nblk * nblk
        sc[row, pl.ds(tail, SLOT_ROWS - tail), :] = jnp.zeros((SLOT_ROWS - tail, width), jnp.bfloat16)

    for copy in small:
        copy.wait()
    own_table()
    load_g0.wait()
    for at, block in own_blocks():
        gr[(col, *at)] = block
    pl.semaphore_wait(barrier, len(near))

    sends = []
    state = {"now": 0.0, "seq": 0, "done": set()}
    link_free, queues, flying = {}, {}, {}
    heap = []
    actions = {}
    pending = []
    ids = {}

    def push(time, kind, name):
        state["seq"] += 1
        heapq.heappush(heap, (time, kind, state["seq"], name))

    def urgency(name):
        if name[0] == "G":
            return name[2]
        return {"S": 0, "C": 1, "L": CH}[name[0]]

    def start(link):
        while queues[link] and flying[link] < WINDOW[link[0]]:
            entry = min(queues[link], key=lambda e: urgency(e[0]))
            queues[link].remove(entry)
            name, src, dst, dev, nbytes, landed, after = entry
            flying[link] += 1
            i = ids.setdefault(name, len(ids))
            copy = pltpu.make_async_remote_copy(
                src_ref=src, dst_ref=dst, send_sem=send_sems.at[i], recv_sem=recv_sems.at[i],
                device_id=dev, device_id_type=MESH,
            )
            copy.start()
            sends.append(copy)
            rate = RATE[link[0]]
            t = max(state["now"], link_free.get(link, 0.0)) + nbytes / rate
            link_free[link] = t
            actions[name] = (functools.partial(arrive, link, i, landed, dev, after), 0.1)
            push(t + HOP, 0, name)

    def arrive(link, i, landed, dev, after):
        pltpu.make_async_remote_copy(
            src_ref=landed, dst_ref=landed, send_sem=send_sems.at[i], recv_sem=recv_sems.at[i],
            device_id=dev, device_id_type=MESH,
        ).wait_recv()
        flying[link] -= 1
        if after is not None:
            after()
        start(link)

    def send(name, src, dst, link, dev, nbytes, landed, after):
        queues.setdefault(link, []).append((name, src, dst, dev, nbytes, landed, after))
        flying.setdefault(link, 0)
        start(link)

    def step(name, needs, fn, cost):
        actions[name] = (fn, cost)
        pending.append((set(needs), name))

    def settle():
        for item in list(pending):
            if item[0] <= state["done"]:
                pending.remove(item)
                push(state["now"], 1, item[1])

    def run():
        settle()
        while heap:
            ready = [e for e in heap if e[0] <= state["now"]]
            e = min(ready, key=lambda e: (e[1], e[0], e[2])) if ready else heap[0]
            heap.remove(e)
            heapq.heapify(heap)
            fn, cost = actions[e[3]]
            state["now"] = max(state["now"], e[0]) + cost
            fn()
            state["done"].add(e[3])
            settle()
        assert not pending, pending

    def z_stream(tag, buf, h):
        half = SPLIT[h] // 2
        nbytes = SPLIT[h] * tile * 2

        def piece(zz, cc, part):
            r = buf.at[wrap(zz, NZ) * 2 + cc]
            if part is None:
                return r.at[pl.ds(STARTS[h], SPLIT[h]), :]
            return r.at[pl.ds(STARTS[h] + part * half, half), :]

        def to_core(name, zz, part):
            src = piece(zz, c, part)
            n = nbytes if part is None else nbytes // 2
            send(name, src, src, ("c", 0), device(dc=1), n, piece(zz, 1 - c, part), None)

        def hop(direction, k):
            part = None if k < NZ // 2 else (0 if direction > 0 else 1)
            src = piece(z - direction * (k - 1), c, part)
            n = nbytes if part is None else nbytes // 2

            def after():
                if k < NZ // 2:
                    hop(direction, k + 1)
                to_core((tag, "c", h, direction, k), z - direction * k, part)

            send((tag, "z", h, direction, k), src, src, ("z", direction), device(dz=direction), n,
                 piece(z - direction * k, c, part), after)

        hop(1, 1)
        hop(-1, 1)
        to_core((tag, "c", h, 0, 0), z, None)

    def z_needs(tag, h, k):
        if k == 0:
            return [(tag, "c", h, 0, 0)]
        return [(tag, s, h, d, k) for s in ("z", "c") for d in (1, -1)]

    def xy_stream(tag, buf, rows, nbytes):
        q = rows // 4

        def piece(dx, dy, half, part):
            r = buf.at[wrap(y + dy, NY) * NX + wrap(x + dx, NX)]
            if part is None:
                return r.at[pl.ds(half * 2 * q, 2 * q), :]
            return r.at[pl.ds((half * 2 + part) * q, q), :]

        def off(half, first, second):
            return (first, second) if half == 0 else (second, first)

        def second_phase(half, at):
            axis = "y" if half == 0 else "x"

            def hop(direction, k):
                part = None if k == 1 else (0 if direction > 0 else 1)
                src = piece(*off(half, at, -direction * (k - 1)), half, part)
                land = piece(*off(half, at, -direction * k), half, part)
                n = nbytes // 2 if k == 1 else nbytes // 4
                name = (tag, half, 2, at, direction, k)
                send(name, src, src, (axis, direction), device(**{"d" + axis: direction}), n, land,
                     (lambda: hop(direction, 2)) if k == 1 else None)

            hop(1, 1)
            hop(-1, 1)

        def first_phase(half):
            axis = "x" if half == 0 else "y"
            far = []

            def hop(direction, k):
                part = None if k == 1 else (0 if direction > 0 else 1)
                src = piece(*off(half, -direction * (k - 1), 0), half, part)
                land = piece(*off(half, -direction * k, 0), half, part)
                n = nbytes // 2 if k == 1 else nbytes // 4
                name = (tag, half, 1, direction, k)

                def after():
                    if k == 1:
                        hop(direction, 2)
                        second_phase(half, -direction)
                    else:
                        far.append(direction)
                        if len(far) == 2:
                            second_phase(half, 2)

                send(name, src, src, (axis, direction), device(**{"d" + axis: direction}), n, land, after)

            hop(1, 1)
            hop(-1, 1)

        for half in (0, 1):
            first_phase(half)
        for half in (0, 1):
            second_phase(half, 0)

    def xy_needs(tag, dx, dy):
        need = []
        for half, (first, second) in enumerate(((dx, dy), (dy, dx))):
            if second == 0:
                need.extend((tag, half, 1, d, abs(first)) for d in ((1, -1) if first == 2 else (-first,)) if first)
            else:
                need.extend((tag, half, 2, first, d, abs(second)) for d in ((1, -1) if second == 2 else (-second,)))
        return need

    def xy_all(tag):
        steps = (0, 1, -1, 2)
        return [n for dx in steps for dy in steps for n in xy_needs(tag, dx, dy)]

    def expand(dxs, dys):
        strip = width // 2

        @pl.loop(0, len(dxs) * len(dys))
        def _(i):
            dx = dxs[0] + (i // len(dys)) * dxs.step
            dy = dys[0] + lax.rem(i, len(dys)) * dys.step
            r = wrap(y + dy, NY) * NX + wrap(x + dx, NX)
            t = sc[r, pl.ds(slots * width, nblk * nblk), :].astype(jnp.float32)
            for u in range(width // strip):
                held = [sc[r, pl.ds(s * width + u * strip, strip), :].reshape(strip // 16, 16, width) for s in range(slots)]
                for b in range(nblk * nblk):
                    line = jnp.broadcast_to(t[b : b + 1, :], (16, width))
                    total = None
                    for s in range(slots):
                        on = jnp.where(line == float(s), 1.0, 0.0).astype(jnp.bfloat16)
                        term = held[s] * on[None]
                        total = term if total is None else total + term
                    at = (b // nblk) * width + u * strip
                    sd[r, pl.ds(at, strip), pl.ds((b % nblk) * width, width)] = total.reshape(strip, width)

    def dots(acc, left_buf, right_buf, k, first, rows):
        n = 2 if k in (0, NZ // 2) else 4
        span = pl.ds(first, rows)

        @pl.loop(0, n)
        def _(i):
            cc = lax.rem(i, 2)
            sign = 1 - 2 * (i // 2)
            t = wrap(z + sign * k, NZ) * 2 + cc
            acc[span, :] += jnp.dot(left_buf[t, span, :], right_buf[t], preferred_element_type=jnp.float32)

    def finish_left(h):
        span = pl.ds(STARTS[h], SPLIT[h])
        lr[col, span, :] = lacc[span, :].astype(jnp.bfloat16)
        z_stream("L", lr, h)

    def finish(h):
        span = pl.ds(STARTS[h], SPLIT[h])
        out_ref[span, :] = cacc[span, :].astype(jnp.bfloat16)

    for h in range(CH):
        z_stream("G", gr, h)
    load_sig.wait()
    xy_stream("S", sc, SLOT_ROWS, SLOT_ROWS * width * 2)
    for at, block in own_blocks():
        gc[(row, *at)] = block
    xy_stream("C", gc, tile, tile * tile * 2)
    for at, block in own_blocks():
        cacc[at] = block.astype(jnp.float32)
    lacc[...] = jnp.zeros_like(lacc)

    zero, near1, pair, two = range(0, 1), range(-1, 2), range(-1, 2, 2), range(2, 3)
    shapes = ((near1, zero), (zero, pair), (pair, pair), (two, range(-1, 3)), (near1, two))
    for i, (dxs, dys) in enumerate(shapes):
        needs = [n for dx in dxs for dy in dys for n in xy_needs("S", dx, dy)]
        step(("expand", i), needs, functools.partial(expand, dxs, dys), 0.3 * len(dxs) * len(dys))
    dense = [("expand", i) for i in range(len(shapes))]
    both = range(CH)
    far = NZ // 2
    for k in range(far):
        for h in both:
            step(("left", h, k), z_needs("G", h, k) + dense,
                 functools.partial(dots, lacc, gr, sd, k, STARTS[h], SPLIT[h]), 0.8)
        needs = [n for h in both for n in z_needs("L", h, k)] + [("left done", h) for h in both]
        step(("prod", k), needs + xy_all("C"), functools.partial(dots, cacc, lr, gc, k, 0, tile), 1.6)
    for h in both:
        step(("left last", h), z_needs("G", h, far) + dense + [("left", h, k) for k in range(far)],
             functools.partial(dots, lacc, gr, sd, far, STARTS[h], SPLIT[h]), 0.6)
        step(("left done", h), [("left last", h)], functools.partial(finish_left, h), 0.3)
        step(("prod last", h), z_needs("L", h, far) + [("prod", k) for k in range(far)],
             functools.partial(dots, cacc, lr, gc, far, STARTS[h], SPLIT[h]), 0.6)
        step(("done", h), [("prod last", h)], functools.partial(finish, h), 0.3)
    run()
    for copy in sends:
        copy.wait_send()
    assert len(ids) == N_COPIES, len(ids)


N_COPIES = 2 * 40 + 2 * CH * (2 * (NZ // 2) * 2 + 1)


def per_device(g0_values, g0_pattern, sigma_values, sigma_pairs, sigma_count):
    tile = g0_values.shape[0]
    _, slots, width, _ = sigma_values.shape
    bf, f32 = jnp.bfloat16, jnp.float32
    hbm = pl.BlockSpec(memory_space=pltpu.HBM)
    return pl.pallas_call(
        kernel,
        name="dyson",
        out_shape=pltpu.VMEM((tile, tile), bf),
        in_specs=[hbm] * 4 + [pl.BlockSpec(memory_space=pltpu.VMEM)],
        out_specs=pl.BlockSpec(memory_space=pltpu.VMEM),
        scratch_shapes=[
            pltpu.SMEM(g0_pattern.shape, jnp.int32),
            pltpu.SMEM((2, slots), jnp.int32),
            pltpu.VMEM((tile, tile), bf),
            pltpu.VMEM((COLS, tile, tile), bf),
            pltpu.VMEM((ROWS, tile, tile), bf),
            pltpu.VMEM((COLS, tile, tile), bf),
            pltpu.VMEM((ROWS, SLOT_ROWS, width), bf),
            pltpu.VMEM((ROWS, tile, tile), bf),
            pltpu.VMEM((tile, tile), f32),
            pltpu.VMEM((tile, tile), f32),
            pltpu.SemaphoreType.DMA((N_COPIES,)),
            pltpu.SemaphoreType.DMA((N_COPIES,)),
            pltpu.SemaphoreType.DMA((5,)),
        ],
        compiler_params=pltpu.CompilerParams(
            collective_id=0, has_side_effects=True, vmem_limit_bytes=58 << 20
        ),
    )(
        g0_values,
        sigma_values.reshape(slots * width, width),
        g0_pattern,
        sigma_pairs.reshape(slots, 2).T,
        sigma_count,
    )


def solution(mesh):
    placed = (
        P("row", "col"),
        P("row", "col"),
        P("row", "col", None, None),
        P("row", "col", None),
        P("row", "col"),
    )
    return jax.shard_map(
        per_device, mesh=mesh, in_specs=placed, out_specs=P("row", "col"), check_vma=False
    )
```

```python
import functools
import heapq

import jax
import jax.numpy as jnp
from jax import lax
from jax.experimental import pallas as pl
from jax.experimental.pallas import tpu as pltpu
from jax.sharding import PartitionSpec as P

MESH = pl.DeviceIdType.MESH
NX, NY, NZ = 4, 4, 8
ROWS = NX * NY
COLS = NZ * 2
SPLIT = (192, 320)
STARTS = (0, 192)
CH = len(SPLIT)
SLOT_ROWS = 832

RATE = {"x": 40.0e3, "y": 40.0e3, "z": 46.0e3, "c": 250.0e3}
HOP = 1.5
WINDOW = {"x": 2, "y": 2, "z": 2, "c": 99}


def kernel(
    g0_ref, sig_ref, pat_hbm, pairs_hbm, count_ref, out_ref,
    pat_ref, pairs_ref, raw, gr, gc, lr, sc, sd, lacc, cacc, send_sems, recv_sems, local_sems,
):
    tile = g0_ref.shape[0]
    width = sig_ref.shape[1]
    nblk = tile // width
    slots = sig_ref.shape[0] // width
    row = lax.axis_index("row")
    col = lax.axis_index("col")
    x, y = lax.rem(row, NX), row // NX
    z, c = col // 2, lax.rem(col, 2)

    def wrap(v, n):
        return lax.rem(v + n, n)

    def device(dx=0, dy=0, dz=0, dc=0):
        xx, yy, zz = wrap(x + dx, NX), wrap(y + dy, NY), wrap(z + dz, NZ)
        cc = 1 - c if dc else c
        return (yy * NX + xx, zz * 2 + cc)

    barrier = pltpu.get_barrier_semaphore()
    near = [device(dx=1), device(dx=-1), device(dy=1), device(dy=-1), device(dz=1), device(dz=-1), device(dc=1)]
    for d in near:
        pl.semaphore_signal(barrier, inc=1, device_id=d, device_id_type=MESH)

    load_g0 = pltpu.make_async_copy(g0_ref, raw, local_sems.at[0])
    load_sig = pltpu.make_async_copy(sig_ref, sc.at[row, pl.ds(0, slots * width), :], local_sems.at[1])
    small = [
        pltpu.make_async_copy(src, dst, local_sems.at[2 + i])
        for i, (src, dst) in enumerate(((pat_hbm, pat_ref), (pairs_hbm, pairs_ref)))
    ]
    for copy in (load_g0, *small, load_sig):
        copy.start()

    def own_blocks():
        for a in range(nblk):
            for b in range(nblk):
                at = (pl.ds(a * width, width), pl.ds(b * width, width))
                block = raw[at]
                yield at, jnp.where(pat_ref[a, b] != 0, block, jnp.zeros_like(block))

    def own_table():
        place = lax.broadcasted_iota(jnp.int32, (nblk * nblk, width), 0)
        count = jnp.broadcast_to(count_ref[...], place.shape)
        table = jnp.full((nblk * nblk, width), -1.0, jnp.float32)
        for s in range(slots):
            at = lax.rem(pairs_ref[0, s], nblk) * nblk + lax.rem(pairs_ref[1, s], nblk)
            table = jnp.where((place == at) & (s < count), float(s), table)
        sc[row, pl.ds(slots * width, nblk * nblk), :] = table.astype(jnp.bfloat16)
        tail = slots * width + nblk * nblk
        sc[row, pl.ds(tail, SLOT_ROWS - tail), :] = jnp.zeros((SLOT_ROWS - tail, width), jnp.bfloat16)

    for copy in small:
        copy.wait()
    load_g0.wait()
    for at, block in own_blocks():
        gr[(col, *at)] = block
    pl.semaphore_wait(barrier, len(near))

    sends = {}
    state = {"now": 0.0, "seq": 0, "done": set()}
    link_free, queues, flying, landed_on = {}, {}, {}, {}
    heap = []
    actions = {}
    pending = []
    ids = {}

    def push(time, kind, name):
        state["seq"] += 1
        heapq.heappush(heap, (time, kind, state["seq"], name))

    def urgency(name):
        if name[0] == "G":
            return name[2]
        return {"S": 0, "C": 1, "L": CH}[name[0]]

    def start(link):
        while queues[link] and flying[link] < WINDOW[link[0]]:
            entry = min(queues[link], key=lambda e: urgency(e[0]))
            queues[link].remove(entry)
            name, src, dst, dev, nbytes, landed, after = entry
            flying[link] += 1
            i = ids.setdefault(name, len(ids))
            copy = pltpu.make_async_remote_copy(
                src_ref=src, dst_ref=dst, send_sem=send_sems.at[i], recv_sem=recv_sems.at[i],
                device_id=dev, device_id_type=MESH,
            )
            copy.start()
            sends[link].append(copy)
            rate = RATE[link[0]]
            t = max(state["now"], link_free.get(link, 0.0)) + nbytes / rate
            link_free[link] = t
            actions[name] = (functools.partial(arrive, link, i, landed, dev, after), 0.1)
            push(t + HOP, 0, name)

    def arrive(link, i, landed, dev, after):
        pltpu.make_async_remote_copy(
            src_ref=landed, dst_ref=landed, send_sem=send_sems.at[i], recv_sem=recv_sems.at[i],
            device_id=dev, device_id_type=MESH,
        ).wait_recv()
        flying[link] -= 1
        landed_on[link] = landed_on.get(link, 0) + 1
        if after is not None:
            after()
        start(link)
        if landed_on[link] > 2:
            sends[link].pop(0).wait_send()

    def send(name, src, dst, link, dev, nbytes, landed, after):
        queues.setdefault(link, []).append((name, src, dst, dev, nbytes, landed, after))
        flying.setdefault(link, 0)
        sends.setdefault(link, [])
        start(link)

    def step(name, needs, fn, cost):
        actions[name] = (fn, cost)
        pending.append((set(needs), name))

    def settle():
        for item in list(pending):
            if item[0] <= state["done"]:
                pending.remove(item)
                push(state["now"], 1, item[1])

    def run():
        settle()
        while heap:
            ready = [e for e in heap if e[0] <= state["now"]]
            e = min(ready, key=lambda e: (e[1], e[0], e[2])) if ready else heap[0]
            heap.remove(e)
            heapq.heapify(heap)
            fn, cost = actions[e[3]]
            state["now"] = max(state["now"], e[0]) + cost
            fn()
            state["done"].add(e[3])
            settle()
        assert not pending, pending

    def z_stream(tag, buf, h):
        half = SPLIT[h] // 2
        nbytes = SPLIT[h] * tile * 2

        def piece(zz, cc, part):
            r = buf.at[wrap(zz, NZ) * 2 + cc]
            if part is None:
                return r.at[pl.ds(STARTS[h], SPLIT[h]), :]
            return r.at[pl.ds(STARTS[h] + part * half, half), :]

        def to_core(name, zz, part):
            src = piece(zz, c, part)
            n = nbytes if part is None else nbytes // 2
            send(name, src, src, ("c", 0), device(dc=1), n, piece(zz, 1 - c, part), None)

        def hop(direction, k):
            part = None if k < NZ // 2 else (0 if direction > 0 else 1)
            src = piece(z - direction * (k - 1), c, part)
            n = nbytes if part is None else nbytes // 2

            def after():
                if k < NZ // 2:
                    hop(direction, k + 1)
                to_core((tag, "c", h, direction, k), z - direction * k, part)

            send((tag, "z", h, direction, k), src, src, ("z", direction), device(dz=direction), n,
                 piece(z - direction * k, c, part), after)

        hop(1, 1)
        hop(-1, 1)
        to_core((tag, "c", h, 0, 0), z, None)

    def z_needs(tag, h, k):
        if k == 0:
            return [(tag, "c", h, 0, 0)]
        return [(tag, s, h, d, k) for s in ("z", "c") for d in (1, -1)]

    def xy_stream(tag, buf, rows, nbytes):
        q = rows // 4

        def piece(dx, dy, half, part):
            r = buf.at[wrap(y + dy, NY) * NX + wrap(x + dx, NX)]
            if part is None:
                return r.at[pl.ds(half * 2 * q, 2 * q), :]
            return r.at[pl.ds((half * 2 + part) * q, q), :]

        def off(half, first, second):
            return (first, second) if half == 0 else (second, first)

        def second_phase(half, at):
            axis = "y" if half == 0 else "x"

            def hop(direction, k):
                part = None if k == 1 else (0 if direction > 0 else 1)
                src = piece(*off(half, at, -direction * (k - 1)), half, part)
                land = piece(*off(half, at, -direction * k), half, part)
                n = nbytes // 2 if k == 1 else nbytes // 4
                name = (tag, half, 2, at, direction, k)
                send(name, src, src, (axis, direction), device(**{"d" + axis: direction}), n, land,
                     (lambda: hop(direction, 2)) if k == 1 else None)

            hop(1, 1)
            hop(-1, 1)

        def first_phase(half):
            axis = "x" if half == 0 else "y"
            far = []

            def hop(direction, k):
                part = None if k == 1 else (0 if direction > 0 else 1)
                src = piece(*off(half, -direction * (k - 1), 0), half, part)
                land = piece(*off(half, -direction * k, 0), half, part)
                n = nbytes // 2 if k == 1 else nbytes // 4
                name = (tag, half, 1, direction, k)

                def after():
                    if k == 1:
                        hop(direction, 2)
                        second_phase(half, -direction)
                    else:
                        far.append(direction)
                        if len(far) == 2:
                            second_phase(half, 2)

                send(name, src, src, (axis, direction), device(**{"d" + axis: direction}), n, land, after)

            hop(1, 1)
            hop(-1, 1)

        for half in (0, 1):
            first_phase(half)
        for half in (0, 1):
            second_phase(half, 0)

    def xy_needs(tag, dx, dy):
        need = []
        for half, (first, second) in enumerate(((dx, dy), (dy, dx))):
            if second == 0:
                need.extend((tag, half, 1, d, abs(first)) for d in ((1, -1) if first == 2 else (-first,)) if first)
            else:
                need.extend((tag, half, 2, first, d, abs(second)) for d in ((1, -1) if second == 2 else (-second,)))
        return need

    def xy_all(tag):
        steps = (0, 1, -1, 2)
        return [n for dx in steps for dy in steps for n in xy_needs(tag, dx, dy)]

    def expand(dxs, dys):
        strip = width // 2

        @pl.loop(0, len(dxs) * len(dys))
        def _(i):
            dx = dxs[0] + (i // len(dys)) * dxs.step
            dy = dys[0] + lax.rem(i, len(dys)) * dys.step
            r = wrap(y + dy, NY) * NX + wrap(x + dx, NX)
            t = sc[r, pl.ds(slots * width, nblk * nblk), :].astype(jnp.float32)
            for u in range(width // strip):
                held = [sc[r, pl.ds(s * width + u * strip, strip), :].reshape(strip // 16, 16, width) for s in range(slots)]
                for b in range(nblk * nblk):
                    line = jnp.broadcast_to(t[b : b + 1, :], (16, width))
                    total = None
                    for s in range(slots):
                        on = jnp.where(line == float(s), 1.0, 0.0).astype(jnp.bfloat16)
                        term = held[s] * on[None]
                        total = term if total is None else total + term
                    at = (b // nblk) * width + u * strip
                    sd[r, pl.ds(at, strip), pl.ds((b % nblk) * width, width)] = total.reshape(strip, width)

    def far_dot(acc, left_buf, right_buf, cc, h):
        span = pl.ds(STARTS[h], SPLIT[h])
        t = wrap(z + NZ // 2, NZ) * 2 + cc
        acc[span, :] += jnp.dot(left_buf[t, span, :], right_buf[t], preferred_element_type=jnp.float32)

    def dots(acc, left_buf, right_buf, k, first, rows):
        n = 2 if k == 0 else 4
        span = pl.ds(first, rows)

        @pl.loop(0, n)
        def _(i):
            cc = lax.rem(i, 2)
            sign = 1 - 2 * (i // 2)
            t = wrap(z + sign * k, NZ) * 2 + cc
            acc[span, :] += jnp.dot(left_buf[t, span, :], right_buf[t], preferred_element_type=jnp.float32)

    def finish_left(h):
        span = pl.ds(STARTS[h], SPLIT[h])
        lr[col, span, :] = lacc[span, :].astype(jnp.bfloat16)
        z_stream("L", lr, h)

    def finish(h):
        span = pl.ds(STARTS[h], SPLIT[h])
        out_ref[span, :] = cacc[span, :].astype(jnp.bfloat16)

    for h in range(CH):
        z_stream("G", gr, h)
    own_table()
    load_sig.wait()
    xy_stream("S", sc, SLOT_ROWS, SLOT_ROWS * width * 2)
    for at, block in own_blocks():
        gc[(row, *at)] = block
    xy_stream("C", gc, tile, tile * tile * 2)
    for at, block in own_blocks():
        cacc[at] = block.astype(jnp.float32)
    lacc[...] = jnp.zeros_like(lacc)

    zero, near1, pair, two = range(0, 1), range(-1, 2), range(-1, 2, 2), range(2, 3)
    shapes = ((near1, zero), (zero, pair), (pair, pair), (two, range(-1, 3)), (near1, two))
    for i, (dxs, dys) in enumerate(shapes):
        needs = [n for dx in dxs for dy in dys for n in xy_needs("S", dx, dy)]
        step(("expand", i), needs, functools.partial(expand, dxs, dys), 0.3 * len(dxs) * len(dys))
    dense = [("expand", i) for i in range(len(shapes))]
    both = range(CH)
    far = NZ // 2
    for k in range(far):
        for h in both:
            step(("left", h, k), z_needs("G", h, k) + dense,
                 functools.partial(dots, lacc, gr, sd, k, STARTS[h], SPLIT[h]), 0.8)
        needs = [n for h in both for n in z_needs("L", h, k)] + [("left done", h) for h in both]
        step(("prod", k), needs + xy_all("C"), functools.partial(dots, cacc, lr, gc, k, 0, tile), 1.6)
    for h in both:
        for who, cc in (("z", c), ("c", 1 - c)):
            got = [("G", who, h, d, far) for d in (1, -1)]
            step(("left last", h, who), got + dense + [("left", h, k) for k in range(far)],
                 functools.partial(far_dot, lacc, gr, sd, cc, h), 0.4)
            got = [("L", who, h, d, far) for d in (1, -1)]
            step(("prod last", h, who), got + [("prod", k) for k in range(far)],
                 functools.partial(far_dot, cacc, lr, gc, cc, h), 0.4)
        step(("left done", h), [("left last", h, who) for who in ("z", "c")], functools.partial(finish_left, h), 0.3)
        step(("done", h), [("prod last", h, who) for who in ("z", "c")], functools.partial(finish, h), 0.3)
    run()
    for left_over in sends.values():
        for copy in left_over:
            copy.wait_send()
    assert len(ids) == N_COPIES, len(ids)


N_COPIES = 2 * 40 + 2 * CH * (2 * (NZ // 2) * 2 + 1)


def per_device(g0_values, g0_pattern, sigma_values, sigma_pairs, sigma_count):
    tile = g0_values.shape[0]
    _, slots, width, _ = sigma_values.shape
    bf, f32 = jnp.bfloat16, jnp.float32
    hbm = pl.BlockSpec(memory_space=pltpu.HBM)
    return pl.pallas_call(
        kernel,
        name="dyson",
        out_shape=pltpu.VMEM((tile, tile), bf),
        in_specs=[hbm] * 4 + [pl.BlockSpec(memory_space=pltpu.VMEM)],
        out_specs=pl.BlockSpec(memory_space=pltpu.VMEM),
        scratch_shapes=[
            pltpu.SMEM(g0_pattern.shape, jnp.int32),
            pltpu.SMEM((2, slots), jnp.int32),
            pltpu.VMEM((tile, tile), bf),
            pltpu.VMEM((COLS, tile, tile), bf),
            pltpu.VMEM((ROWS, tile, tile), bf),
            pltpu.VMEM((COLS, tile, tile), bf),
            pltpu.VMEM((ROWS, SLOT_ROWS, width), bf),
            pltpu.VMEM((ROWS, tile, tile), bf),
            pltpu.VMEM((tile, tile), f32),
            pltpu.VMEM((tile, tile), f32),
            pltpu.SemaphoreType.DMA((N_COPIES,)),
            pltpu.SemaphoreType.DMA((N_COPIES,)),
            pltpu.SemaphoreType.DMA((5,)),
        ],
        compiler_params=pltpu.CompilerParams(
            collective_id=0, has_side_effects=True, vmem_limit_bytes=58 << 20
        ),
    )(
        g0_values,
        sigma_values.reshape(slots * width, width),
        g0_pattern,
        sigma_pairs.reshape(slots, 2).T,
        sigma_count,
    )


def solution(mesh):
    placed = (
        P("row", "col"),
        P("row", "col"),
        P("row", "col", None, None),
        P("row", "col", None),
        P("row", "col"),
    )
    return jax.shard_map(
        per_device, mesh=mesh, in_specs=placed, out_specs=P("row", "col"), check_vma=False
    )
```

```python
import functools
import heapq

import jax
import jax.numpy as jnp
from jax import lax
from jax.experimental import pallas as pl
from jax.experimental.pallas import tpu as pltpu
from jax.sharding import PartitionSpec as P

MESH = pl.DeviceIdType.MESH
NX, NY, NZ = 4, 4, 8
ROWS = NX * NY
COLS = NZ * 2
SPLIT = (224, 288)
STARTS = (0, 224)
CH = len(SPLIT)
SLOT_ROWS = 832

RATE = {"x": 40.0e3, "y": 40.0e3, "z": 46.0e3, "c": 250.0e3}
HOP = 1.5
WINDOW = {"x": 2, "y": 2, "z": 2, "c": 99}


def kernel(
    g0_ref, sig_ref, pat_hbm, pairs_hbm, count_ref, out_ref,
    pat_ref, pairs_ref, raw, gr, gc, lr, sc, sd, lacc, cacc, send_sems, recv_sems, local_sems,
):
    tile = g0_ref.shape[0]
    width = sig_ref.shape[1]
    nblk = tile // width
    slots = sig_ref.shape[0] // width
    row = lax.axis_index("row")
    col = lax.axis_index("col")
    x, y = lax.rem(row, NX), row // NX
    z, c = col // 2, lax.rem(col, 2)

    def wrap(v, n):
        return lax.rem(v + n, n)

    def device(dx=0, dy=0, dz=0, dc=0):
        xx, yy, zz = wrap(x + dx, NX), wrap(y + dy, NY), wrap(z + dz, NZ)
        cc = 1 - c if dc else c
        return (yy * NX + xx, zz * 2 + cc)

    barrier = pltpu.get_barrier_semaphore()
    near = [device(dx=1), device(dx=-1), device(dy=1), device(dy=-1), device(dz=1), device(dz=-1), device(dc=1)]
    for d in near:
        pl.semaphore_signal(barrier, inc=1, device_id=d, device_id_type=MESH)

    top = tile // 2
    load_g0 = [
        pltpu.make_async_copy(g0_ref.at[pl.ds(i * top, top), :], raw.at[pl.ds(i * top, top), :], local_sems.at[i])
        for i in range(2)
    ]
    load_sig = pltpu.make_async_copy(sig_ref, sc.at[row, pl.ds(0, slots * width), :], local_sems.at[4])
    small = [
        pltpu.make_async_copy(src, dst, local_sems.at[2 + i])
        for i, (src, dst) in enumerate(((pat_hbm, pat_ref), (pairs_hbm, pairs_ref)))
    ]
    for copy in (load_g0[0], *small, load_g0[1], load_sig):
        copy.start()

    def own_blocks(block_rows=range(nblk)):
        for a in block_rows:
            for b in range(nblk):
                at = (pl.ds(a * width, width), pl.ds(b * width, width))
                block = raw[at]
                yield at, jnp.where(pat_ref[a, b] != 0, block, jnp.zeros_like(block))

    def own_table():
        place = lax.broadcasted_iota(jnp.int32, (nblk * nblk, width), 0)
        count = jnp.broadcast_to(count_ref[...], place.shape)
        table = jnp.full((nblk * nblk, width), -1.0, jnp.float32)
        for s in range(slots):
            at = lax.rem(pairs_ref[0, s], nblk) * nblk + lax.rem(pairs_ref[1, s], nblk)
            table = jnp.where((place == at) & (s < count), float(s), table)
        sc[row, pl.ds(slots * width, nblk * nblk), :] = table.astype(jnp.bfloat16)
        tail = slots * width + nblk * nblk
        sc[row, pl.ds(tail, SLOT_ROWS - tail), :] = jnp.zeros((SLOT_ROWS - tail, width), jnp.bfloat16)

    for copy in small:
        copy.wait()
    load_g0[0].wait()
    for at, block in own_blocks(range(nblk // 2)):
        gr[(col, *at)] = block
    pl.semaphore_wait(barrier, len(near))

    sends = {}
    state = {"now": 0.0, "seq": 0, "done": set()}
    link_free, queues, flying, landed_on = {}, {}, {}, {}
    heap = []
    actions = {}
    pending = []
    ids = {}

    def push(time, kind, name):
        state["seq"] += 1
        heapq.heappush(heap, (time, kind, state["seq"], name))

    def urgency(name):
        if name[0] == "G":
            return name[2]
        return {"S": 0, "C": 1, "L": CH}[name[0]]

    def start(link):
        while queues[link] and flying[link] < WINDOW[link[0]]:
            entry = min(queues[link], key=lambda e: urgency(e[0]))
            queues[link].remove(entry)
            name, src, dst, dev, nbytes, landed, after = entry
            flying[link] += 1
            i = ids.setdefault(name, len(ids))
            copy = pltpu.make_async_remote_copy(
                src_ref=src, dst_ref=dst, send_sem=send_sems.at[i], recv_sem=recv_sems.at[i],
                device_id=dev, device_id_type=MESH,
            )
            copy.start()
            sends[link].append(copy)
            rate = RATE[link[0]]
            t = max(state["now"], link_free.get(link, 0.0)) + nbytes / rate
            link_free[link] = t
            actions[name] = (functools.partial(arrive, link, i, landed, dev, after), 0.1)
            push(t + HOP, 0, name)

    def arrive(link, i, landed, dev, after):
        pltpu.make_async_remote_copy(
            src_ref=landed, dst_ref=landed, send_sem=send_sems.at[i], recv_sem=recv_sems.at[i],
            device_id=dev, device_id_type=MESH,
        ).wait_recv()
        flying[link] -= 1
        landed_on[link] = landed_on.get(link, 0) + 1
        if after is not None:
            after()
        start(link)
        if landed_on[link] > 2:
            sends[link].pop(0).wait_send()

    def send(name, src, dst, link, dev, nbytes, landed, after):
        queues.setdefault(link, []).append((name, src, dst, dev, nbytes, landed, after))
        flying.setdefault(link, 0)
        sends.setdefault(link, [])
        start(link)

    def step(name, needs, fn, cost):
        actions[name] = (fn, cost)
        pending.append((set(needs), name))

    def settle():
        for item in list(pending):
            if item[0] <= state["done"]:
                pending.remove(item)
                push(state["now"], 1, item[1])

    def run():
        settle()
        while heap:
            ready = [e for e in heap if e[0] <= state["now"]]
            e = min(ready, key=lambda e: (e[1], e[0], e[2])) if ready else heap[0]
            heap.remove(e)
            heapq.heapify(heap)
            fn, cost = actions[e[3]]
            state["now"] = max(state["now"], e[0]) + cost
            fn()
            state["done"].add(e[3])
            settle()
        assert not pending, pending

    def z_stream(tag, buf, h):
        half = SPLIT[h] // 2
        nbytes = SPLIT[h] * tile * 2

        def piece(zz, cc, part):
            r = buf.at[wrap(zz, NZ) * 2 + cc]
            if part is None:
                return r.at[pl.ds(STARTS[h], SPLIT[h]), :]
            return r.at[pl.ds(STARTS[h] + part * half, half), :]

        def to_core(name, zz, part):
            src = piece(zz, c, part)
            n = nbytes if part is None else nbytes // 2
            send(name, src, src, ("c", 0), device(dc=1), n, piece(zz, 1 - c, part), None)

        def hop(direction, k):
            part = None if k < NZ // 2 else (0 if direction > 0 else 1)
            src = piece(z - direction * (k - 1), c, part)
            n = nbytes if part is None else nbytes // 2

            def after():
                if k < NZ // 2:
                    hop(direction, k + 1)
                to_core((tag, "c", h, direction, k), z - direction * k, part)

            send((tag, "z", h, direction, k), src, src, ("z", direction), device(dz=direction), n,
                 piece(z - direction * k, c, part), after)

        hop(1, 1)
        hop(-1, 1)
        to_core((tag, "c", h, 0, 0), z, None)

    def z_needs(tag, h, k):
        if k == 0:
            return [(tag, "c", h, 0, 0)]
        return [(tag, s, h, d, k) for s in ("z", "c") for d in (1, -1)]

    def xy_stream(tag, buf, rows, nbytes):
        q = rows // 4

        def piece(dx, dy, half, part):
            r = buf.at[wrap(y + dy, NY) * NX + wrap(x + dx, NX)]
            if part is None:
                return r.at[pl.ds(half * 2 * q, 2 * q), :]
            return r.at[pl.ds((half * 2 + part) * q, q), :]

        def off(half, first, second):
            return (first, second) if half == 0 else (second, first)

        def second_phase(half, at):
            axis = "y" if half == 0 else "x"

            def hop(direction, k):
                part = None if k == 1 else (0 if direction > 0 else 1)
                src = piece(*off(half, at, -direction * (k - 1)), half, part)
                land = piece(*off(half, at, -direction * k), half, part)
                n = nbytes // 2 if k == 1 else nbytes // 4
                name = (tag, half, 2, at, direction, k)
                send(name, src, src, (axis, direction), device(**{"d" + axis: direction}), n, land,
                     (lambda: hop(direction, 2)) if k == 1 else None)

            hop(1, 1)
            hop(-1, 1)

        def first_phase(half):
            axis = "x" if half == 0 else "y"
            far = []

            def hop(direction, k):
                part = None if k == 1 else (0 if direction > 0 else 1)
                src = piece(*off(half, -direction * (k - 1), 0), half, part)
                land = piece(*off(half, -direction * k, 0), half, part)
                n = nbytes // 2 if k == 1 else nbytes // 4
                name = (tag, half, 1, direction, k)

                def after():
                    if k == 1:
                        hop(direction, 2)
                        second_phase(half, -direction)
                    else:
                        far.append(direction)
                        if len(far) == 2:
                            second_phase(half, 2)

                send(name, src, src, (axis, direction), device(**{"d" + axis: direction}), n, land, after)

            hop(1, 1)
            hop(-1, 1)

        for half in (0, 1):
            first_phase(half)
        for half in (0, 1):
            second_phase(half, 0)

    def xy_needs(tag, dx, dy):
        need = []
        for half, (first, second) in enumerate(((dx, dy), (dy, dx))):
            if second == 0:
                need.extend((tag, half, 1, d, abs(first)) for d in ((1, -1) if first == 2 else (-first,)) if first)
            else:
                need.extend((tag, half, 2, first, d, abs(second)) for d in ((1, -1) if second == 2 else (-second,)))
        return need

    def xy_all(tag):
        steps = (0, 1, -1, 2)
        return [n for dx in steps for dy in steps for n in xy_needs(tag, dx, dy)]

    def expand(dxs, dys):
        strip = width // 2

        @pl.loop(0, len(dxs) * len(dys))
        def _(i):
            dx = dxs[0] + (i // len(dys)) * dxs.step
            dy = dys[0] + lax.rem(i, len(dys)) * dys.step
            r = wrap(y + dy, NY) * NX + wrap(x + dx, NX)
            t = sc[r, pl.ds(slots * width, nblk * nblk), :].astype(jnp.float32)
            for u in range(width // strip):
                held = [sc[r, pl.ds(s * width + u * strip, strip), :].reshape(strip // 16, 16, width) for s in range(slots)]
                for b in range(nblk * nblk):
                    line = jnp.broadcast_to(t[b : b + 1, :], (16, width))
                    total = None
                    for s in range(slots):
                        on = jnp.where(line == float(s), 1.0, 0.0).astype(jnp.bfloat16)
                        term = held[s] * on[None]
                        total = term if total is None else total + term
                    at = (b // nblk) * width + u * strip
                    sd[r, pl.ds(at, strip), pl.ds((b % nblk) * width, width)] = total.reshape(strip, width)

    def far_dot(acc, left_buf, right_buf, cc, h):
        span = pl.ds(STARTS[h], SPLIT[h])
        t = wrap(z + NZ // 2, NZ) * 2 + cc
        acc[span, :] += jnp.dot(left_buf[t, span, :], right_buf[t], preferred_element_type=jnp.float32)

    def dots(acc, left_buf, right_buf, k, first, rows):
        n = 2 if k == 0 else 4
        span = pl.ds(first, rows)

        @pl.loop(0, n)
        def _(i):
            cc = lax.rem(i, 2)
            sign = 1 - 2 * (i // 2)
            t = wrap(z + sign * k, NZ) * 2 + cc
            acc[span, :] += jnp.dot(left_buf[t, span, :], right_buf[t], preferred_element_type=jnp.float32)

    def finish_left(h):
        span = pl.ds(STARTS[h], SPLIT[h])
        lr[col, span, :] = lacc[span, :].astype(jnp.bfloat16)
        z_stream("L", lr, h)

    def finish(h):
        span = pl.ds(STARTS[h], SPLIT[h])
        out_ref[span, :] = cacc[span, :].astype(jnp.bfloat16)

    z_stream("G", gr, 0)
    load_g0[1].wait()
    for at, block in own_blocks(range(nblk // 2, nblk)):
        gr[(col, *at)] = block
    z_stream("G", gr, 1)
    own_table()
    load_sig.wait()
    xy_stream("S", sc, SLOT_ROWS, SLOT_ROWS * width * 2)
    for at, block in own_blocks():
        gc[(row, *at)] = block
    xy_stream("C", gc, tile, tile * tile * 2)
    for at, block in own_blocks():
        cacc[at] = block.astype(jnp.float32)
    lacc[...] = jnp.zeros_like(lacc)

    zero, near1, pair, two = range(0, 1), range(-1, 2), range(-1, 2, 2), range(2, 3)
    shapes = ((near1, zero), (zero, pair), (pair, pair), (two, range(-1, 3)), (near1, two))
    for i, (dxs, dys) in enumerate(shapes):
        needs = [n for dx in dxs for dy in dys for n in xy_needs("S", dx, dy)]
        step(("expand", i), needs, functools.partial(expand, dxs, dys), 0.3 * len(dxs) * len(dys))
    dense = [("expand", i) for i in range(len(shapes))]
    both = range(CH)
    far = NZ // 2
    for k in range(far):
        for h in both:
            step(("left", h, k), z_needs("G", h, k) + dense,
                 functools.partial(dots, lacc, gr, sd, k, STARTS[h], SPLIT[h]), 0.8)
        needs = [n for h in both for n in z_needs("L", h, k)] + [("left done", h) for h in both]
        step(("prod", k), needs + xy_all("C"), functools.partial(dots, cacc, lr, gc, k, 0, tile), 1.6)
    for h in both:
        for who, cc in (("z", c), ("c", 1 - c)):
            got = [("G", who, h, d, far) for d in (1, -1)]
            step(("left last", h, who), got + dense + [("left", h, k) for k in range(far)],
                 functools.partial(far_dot, lacc, gr, sd, cc, h), 0.4)
            got = [("L", who, h, d, far) for d in (1, -1)]
            step(("prod last", h, who), got + [("prod", k) for k in range(far)],
                 functools.partial(far_dot, cacc, lr, gc, cc, h), 0.4)
        step(("left done", h), [("left last", h, who) for who in ("z", "c")], functools.partial(finish_left, h), 0.3)
        step(("done", h), [("prod last", h, who) for who in ("z", "c")], functools.partial(finish, h), 0.3)
    run()
    for left_over in sends.values():
        for copy in left_over:
            copy.wait_send()
    assert len(ids) == N_COPIES, len(ids)


N_COPIES = 2 * 40 + 2 * CH * (2 * (NZ // 2) * 2 + 1)


def per_device(g0_values, g0_pattern, sigma_values, sigma_pairs, sigma_count):
    tile = g0_values.shape[0]
    _, slots, width, _ = sigma_values.shape
    bf, f32 = jnp.bfloat16, jnp.float32
    hbm = pl.BlockSpec(memory_space=pltpu.HBM)
    return pl.pallas_call(
        kernel,
        name="dyson",
        out_shape=pltpu.VMEM((tile, tile), bf),
        in_specs=[hbm] * 4 + [pl.BlockSpec(memory_space=pltpu.VMEM)],
        out_specs=pl.BlockSpec(memory_space=pltpu.VMEM),
        scratch_shapes=[
            pltpu.SMEM(g0_pattern.shape, jnp.int32),
            pltpu.SMEM((2, slots), jnp.int32),
            pltpu.VMEM((tile, tile), bf),
            pltpu.VMEM((COLS, tile, tile), bf),
            pltpu.VMEM((ROWS, tile, tile), bf),
            pltpu.VMEM((COLS, tile, tile), bf),
            pltpu.VMEM((ROWS, SLOT_ROWS, width), bf),
            pltpu.VMEM((ROWS, tile, tile), bf),
            pltpu.VMEM((tile, tile), f32),
            pltpu.VMEM((tile, tile), f32),
            pltpu.SemaphoreType.DMA((N_COPIES,)),
            pltpu.SemaphoreType.DMA((N_COPIES,)),
            pltpu.SemaphoreType.DMA((5,)),
        ],
        compiler_params=pltpu.CompilerParams(
            collective_id=0, has_side_effects=True, vmem_limit_bytes=58 << 20
        ),
    )(
        g0_values,
        sigma_values.reshape(slots * width, width),
        g0_pattern,
        sigma_pairs.reshape(slots, 2).T,
        sigma_count,
    )


def solution(mesh):
    placed = (
        P("row", "col"),
        P("row", "col"),
        P("row", "col", None, None),
        P("row", "col", None),
        P("row", "col"),
    )
    return jax.shard_map(
        per_device, mesh=mesh, in_specs=placed, out_specs=P("row", "col"), check_vma=False
    )
```

```python
import functools
import heapq

import jax
import jax.numpy as jnp
from jax import lax
from jax.experimental import pallas as pl
from jax.experimental.pallas import tpu as pltpu
from jax.sharding import PartitionSpec as P

MESH = pl.DeviceIdType.MESH
NX, NY, NZ = 4, 4, 8
ROWS = NX * NY
COLS = NZ * 2
SPLIT = (224, 288)
STARTS = (0, 224)
CH = len(SPLIT)
SLOT_ROWS = 832

RATE = {"x": 40.0e3, "y": 40.0e3, "z": 46.0e3, "c": 250.0e3}
HOP = 1.5
WINDOW = {"x": 2, "y": 2, "z": 2, "c": 99}


def kernel(
    g0_ref, sig_ref, pat_hbm, pairs_hbm, count_ref, out_ref,
    pat_ref, pairs_ref, raw, gr, gc, lr, sc, sd, lacc, cacc, send_sems, recv_sems, local_sems,
):
    tile = g0_ref.shape[0]
    width = sig_ref.shape[1]
    nblk = tile // width
    slots = sig_ref.shape[0] // width
    row = lax.axis_index("row")
    col = lax.axis_index("col")
    x, y = lax.rem(row, NX), row // NX
    z, c = col // 2, lax.rem(col, 2)

    def wrap(v, n):
        return lax.rem(v + n, n)

    def device(dx=0, dy=0, dz=0, dc=0):
        xx, yy, zz = wrap(x + dx, NX), wrap(y + dy, NY), wrap(z + dz, NZ)
        cc = 1 - c if dc else c
        return (yy * NX + xx, zz * 2 + cc)

    barrier = pltpu.get_barrier_semaphore()
    near = [device(dx=1), device(dx=-1), device(dy=1), device(dy=-1), device(dz=1), device(dz=-1), device(dc=1)]
    for d in near:
        pl.semaphore_signal(barrier, inc=1, device_id=d, device_id_type=MESH)

    top = tile // 2
    load_g0 = [
        pltpu.make_async_copy(g0_ref.at[pl.ds(i * top, top), :], raw.at[pl.ds(i * top, top), :], local_sems.at[i])
        for i in range(2)
    ]
    load_sig = pltpu.make_async_copy(sig_ref, sc.at[row, pl.ds(0, slots * width), :], local_sems.at[4])
    small = [
        pltpu.make_async_copy(src, dst, local_sems.at[2 + i])
        for i, (src, dst) in enumerate(((pat_hbm, pat_ref), (pairs_hbm, pairs_ref)))
    ]
    for copy in (load_g0[0], *small, load_g0[1], load_sig):
        copy.start()

    def own_blocks(block_rows=range(nblk)):
        for a in block_rows:
            for b in range(nblk):
                at = (pl.ds(a * width, width), pl.ds(b * width, width))
                block = raw[at]
                yield at, jnp.where(pat_ref[a, b] != 0, block, jnp.zeros_like(block))

    def own_table():
        place = lax.broadcasted_iota(jnp.int32, (nblk * nblk, width), 0)
        count = jnp.broadcast_to(count_ref[...], place.shape)
        table = jnp.full((nblk * nblk, width), -1.0, jnp.float32)
        for s in range(slots):
            at = lax.rem(pairs_ref[0, s], nblk) * nblk + lax.rem(pairs_ref[1, s], nblk)
            table = jnp.where((place == at) & (s < count), float(s), table)
        sc[row, pl.ds(slots * width, nblk * nblk), :] = table.astype(jnp.bfloat16)
        tail = slots * width + nblk * nblk
        sc[row, pl.ds(tail, SLOT_ROWS - tail), :] = jnp.zeros((SLOT_ROWS - tail, width), jnp.bfloat16)

    for copy in small:
        copy.wait()
    load_g0[0].wait()
    for at, block in own_blocks(range(nblk // 2)):
        gr[(col, *at)] = block
    pl.semaphore_wait(barrier, len(near))

    sends = {}
    state = {"now": 0.0, "seq": 0, "done": set()}
    link_free, queues, flying, landed_on = {}, {}, {}, {}
    heap = []
    actions = {}
    pending = []
    ids = {}

    def push(time, kind, name):
        state["seq"] += 1
        heapq.heappush(heap, (time, kind, state["seq"], name))

    def urgency(name):
        if name[0] == "G":
            return name[2]
        return {"S": 0, "C": 1, "L": CH}[name[0]]

    def start(link):
        while queues[link] and flying[link] < WINDOW[link[0]]:
            entry = min(queues[link], key=lambda e: urgency(e[0]))
            queues[link].remove(entry)
            name, src, dst, dev, nbytes, landed, after = entry
            flying[link] += 1
            i = ids.setdefault(name, len(ids))
            copy = pltpu.make_async_remote_copy(
                src_ref=src, dst_ref=dst, send_sem=send_sems.at[i], recv_sem=recv_sems.at[i],
                device_id=dev, device_id_type=MESH,
            )
            copy.start()
            sends[link].append(copy)
            rate = RATE[link[0]]
            t = max(state["now"], link_free.get(link, 0.0)) + nbytes / rate
            link_free[link] = t
            actions[name] = (functools.partial(arrive, link, i, landed, dev, after), 0.1)
            push(t + HOP, 0, name)

    def arrive(link, i, landed, dev, after):
        pltpu.make_async_remote_copy(
            src_ref=landed, dst_ref=landed, send_sem=send_sems.at[i], recv_sem=recv_sems.at[i],
            device_id=dev, device_id_type=MESH,
        ).wait_recv()
        flying[link] -= 1
        landed_on[link] = landed_on.get(link, 0) + 1
        if after is not None:
            after()
        start(link)
        if landed_on[link] > 2:
            sends[link].pop(0).wait_send()

    def send(name, src, dst, link, dev, nbytes, landed, after):
        queues.setdefault(link, []).append((name, src, dst, dev, nbytes, landed, after))
        flying.setdefault(link, 0)
        sends.setdefault(link, [])
        start(link)

    def step(name, needs, fn, cost):
        actions[name] = (fn, cost)
        pending.append((set(needs), name))

    def settle():
        for item in list(pending):
            if item[0] <= state["done"]:
                pending.remove(item)
                push(state["now"], 1, item[1])

    def run():
        settle()
        while heap:
            ready = [e for e in heap if e[0] <= state["now"]]
            e = min(ready, key=lambda e: (e[1], e[0], e[2])) if ready else heap[0]
            heap.remove(e)
            heapq.heapify(heap)
            fn, cost = actions[e[3]]
            state["now"] = max(state["now"], e[0]) + cost
            fn()
            state["done"].add(e[3])
            settle()
        assert not pending, pending

    def z_stream(tag, buf, h):
        half = SPLIT[h] // 2
        nbytes = SPLIT[h] * tile * 2

        def piece(zz, cc, part):
            r = buf.at[wrap(zz, NZ) * 2 + cc]
            if part is None:
                return r.at[pl.ds(STARTS[h], SPLIT[h]), :]
            return r.at[pl.ds(STARTS[h] + part * half, half), :]

        def to_core(name, zz, part, first=0, rows=None):
            src, land = piece(zz, c, part), piece(zz, 1 - c, part)
            if rows is not None:
                src, land = src.at[pl.ds(first, rows), :], land.at[pl.ds(first, rows), :]
            n = (rows or SPLIT[h]) * tile * 2
            send(name, src, src, ("c", 0), device(dc=1), n, land, None)

        def hop(direction, k):
            part = None if k < NZ // 2 else (0 if direction > 0 else 1)
            src = piece(z - direction * (k - 1), c, part)
            n = nbytes if part is None else nbytes // 2

            def after():
                if k < NZ // 2:
                    hop(direction, k + 1)
                if part is None:
                    to_core((tag, "c", h, direction, k), z - direction * k, part)
                else:
                    cut = half // 32 * 16
                    to_core((tag, "c", h, direction, k), z - direction * k, part, 0, cut)
                    to_core((tag, "c2", h, direction, k), z - direction * k, part, cut, half - cut)

            send((tag, "z", h, direction, k), src, src, ("z", direction), device(dz=direction), n,
                 piece(z - direction * k, c, part), after)

        hop(1, 1)
        hop(-1, 1)
        to_core((tag, "c", h, 0, 0), z, None)

    def z_needs(tag, h, k):
        if k == 0:
            return [(tag, "c", h, 0, 0)]
        return [(tag, s, h, d, k) for s in ("z", "c") for d in (1, -1)]

    def xy_stream(tag, buf, rows, nbytes):
        q = rows // 4

        def piece(dx, dy, half, part):
            r = buf.at[wrap(y + dy, NY) * NX + wrap(x + dx, NX)]
            if part is None:
                return r.at[pl.ds(half * 2 * q, 2 * q), :]
            return r.at[pl.ds((half * 2 + part) * q, q), :]

        def off(half, first, second):
            return (first, second) if half == 0 else (second, first)

        def second_phase(half, at):
            axis = "y" if half == 0 else "x"

            def hop(direction, k):
                part = None if k == 1 else (0 if direction > 0 else 1)
                src = piece(*off(half, at, -direction * (k - 1)), half, part)
                land = piece(*off(half, at, -direction * k), half, part)
                n = nbytes // 2 if k == 1 else nbytes // 4
                name = (tag, half, 2, at, direction, k)
                send(name, src, src, (axis, direction), device(**{"d" + axis: direction}), n, land,
                     (lambda: hop(direction, 2)) if k == 1 else None)

            hop(1, 1)
            hop(-1, 1)

        def first_phase(half):
            axis = "x" if half == 0 else "y"
            far = []

            def hop(direction, k):
                part = None if k == 1 else (0 if direction > 0 else 1)
                src = piece(*off(half, -direction * (k - 1), 0), half, part)
                land = piece(*off(half, -direction * k, 0), half, part)
                n = nbytes // 2 if k == 1 else nbytes // 4
                name = (tag, half, 1, direction, k)

                def after():
                    if k == 1:
                        hop(direction, 2)
                        second_phase(half, -direction)
                    else:
                        far.append(direction)
                        if len(far) == 2:
                            second_phase(half, 2)

                send(name, src, src, (axis, direction), device(**{"d" + axis: direction}), n, land, after)

            hop(1, 1)
            hop(-1, 1)

        for half in (0, 1):
            first_phase(half)
        for half in (0, 1):
            second_phase(half, 0)

    def xy_needs(tag, dx, dy):
        need = []
        for half, (first, second) in enumerate(((dx, dy), (dy, dx))):
            if second == 0:
                need.extend((tag, half, 1, d, abs(first)) for d in ((1, -1) if first == 2 else (-first,)) if first)
            else:
                need.extend((tag, half, 2, first, d, abs(second)) for d in ((1, -1) if second == 2 else (-second,)))
        return need

    def xy_all(tag):
        steps = (0, 1, -1, 2)
        return [n for dx in steps for dy in steps for n in xy_needs(tag, dx, dy)]

    def expand(dxs, dys):
        strip = width // 2

        @pl.loop(0, len(dxs) * len(dys))
        def _(i):
            dx = dxs[0] + (i // len(dys)) * dxs.step
            dy = dys[0] + lax.rem(i, len(dys)) * dys.step
            r = wrap(y + dy, NY) * NX + wrap(x + dx, NX)
            t = sc[r, pl.ds(slots * width, nblk * nblk), :].astype(jnp.float32)
            for u in range(width // strip):
                held = [sc[r, pl.ds(s * width + u * strip, strip), :].reshape(strip // 16, 16, width) for s in range(slots)]
                for b in range(nblk * nblk):
                    line = jnp.broadcast_to(t[b : b + 1, :], (16, width))
                    total = None
                    for s in range(slots):
                        on = jnp.where(line == float(s), 1.0, 0.0).astype(jnp.bfloat16)
                        term = held[s] * on[None]
                        total = term if total is None else total + term
                    at = (b // nblk) * width + u * strip
                    sd[r, pl.ds(at, strip), pl.ds((b % nblk) * width, width)] = total.reshape(strip, width)

    def far_dot(acc, left_buf, right_buf, cc, h):
        span = pl.ds(STARTS[h], SPLIT[h])
        t = wrap(z + NZ // 2, NZ) * 2 + cc
        acc[span, :] += jnp.dot(left_buf[t, span, :], right_buf[t], preferred_element_type=jnp.float32)

    def dots(acc, left_buf, right_buf, k, first, rows):
        n = 2 if k == 0 else 4
        span = pl.ds(first, rows)

        @pl.loop(0, n)
        def _(i):
            cc = lax.rem(i, 2)
            sign = 1 - 2 * (i // 2)
            t = wrap(z + sign * k, NZ) * 2 + cc
            acc[span, :] += jnp.dot(left_buf[t, span, :], right_buf[t], preferred_element_type=jnp.float32)

    def finish_left(h):
        span = pl.ds(STARTS[h], SPLIT[h])
        lr[col, span, :] = lacc[span, :].astype(jnp.bfloat16)
        z_stream("L", lr, h)

    def finish(h):
        span = pl.ds(STARTS[h], SPLIT[h])
        out_ref[span, :] = cacc[span, :].astype(jnp.bfloat16)

    z_stream("G", gr, 0)
    load_g0[1].wait()
    for at, block in own_blocks(range(nblk // 2, nblk)):
        gr[(col, *at)] = block
    z_stream("G", gr, 1)
    own_table()
    load_sig.wait()
    xy_stream("S", sc, SLOT_ROWS, SLOT_ROWS * width * 2)
    for at, block in own_blocks():
        gc[(row, *at)] = block
    xy_stream("C", gc, tile, tile * tile * 2)
    for at, block in own_blocks():
        cacc[at] = block.astype(jnp.float32)
    lacc[...] = jnp.zeros_like(lacc)

    zero, near1, pair, two = range(0, 1), range(-1, 2), range(-1, 2, 2), range(2, 3)
    shapes = ((near1, zero), (zero, pair), (pair, pair), (two, range(-1, 3)), (near1, two))
    for i, (dxs, dys) in enumerate(shapes):
        needs = [n for dx in dxs for dy in dys for n in xy_needs("S", dx, dy)]
        step(("expand", i), needs, functools.partial(expand, dxs, dys), 0.3 * len(dxs) * len(dys))
    dense = [("expand", i) for i in range(len(shapes))]
    both = range(CH)
    far = NZ // 2
    for k in range(far):
        for h in both:
            step(("left", h, k), z_needs("G", h, k) + dense,
                 functools.partial(dots, lacc, gr, sd, k, STARTS[h], SPLIT[h]), 0.8)
        needs = [n for h in both for n in z_needs("L", h, k)] + [("left done", h) for h in both]
        step(("prod", k), needs + xy_all("C"), functools.partial(dots, cacc, lr, gc, k, 0, tile), 1.6)
    for h in both:
        parts_of = {"z": ("z",), "c": ("c", "c2")}
        for who, cc in (("z", c), ("c", 1 - c)):
            got = [("G", w, h, d, far) for d in (1, -1) for w in parts_of[who]]
            step(("left last", h, who), got + dense + [("left", h, k) for k in range(far)],
                 functools.partial(far_dot, lacc, gr, sd, cc, h), 0.4)
            got = [("L", w, h, d, far) for d in (1, -1) for w in parts_of[who]]
            step(("prod last", h, who), got + [("prod", k) for k in range(far)],
                 functools.partial(far_dot, cacc, lr, gc, cc, h), 0.4)
        step(("left done", h), [("left last", h, who) for who in ("z", "c")], functools.partial(finish_left, h), 0.3)
        step(("done", h), [("prod last", h, who) for who in ("z", "c")], functools.partial(finish, h), 0.3)
    run()
    for left_over in sends.values():
        for copy in left_over:
            copy.wait_send()
    assert len(ids) == N_COPIES, len(ids)


N_COPIES = 2 * 40 + 2 * CH * (2 * (NZ // 2) * 2 + 1 + 2)


def per_device(g0_values, g0_pattern, sigma_values, sigma_pairs, sigma_count):
    tile = g0_values.shape[0]
    _, slots, width, _ = sigma_values.shape
    bf, f32 = jnp.bfloat16, jnp.float32
    hbm = pl.BlockSpec(memory_space=pltpu.HBM)
    return pl.pallas_call(
        kernel,
        name="dyson",
        out_shape=pltpu.VMEM((tile, tile), bf),
        in_specs=[hbm] * 4 + [pl.BlockSpec(memory_space=pltpu.VMEM)],
        out_specs=pl.BlockSpec(memory_space=pltpu.VMEM),
        scratch_shapes=[
            pltpu.SMEM(g0_pattern.shape, jnp.int32),
            pltpu.SMEM((2, slots), jnp.int32),
            pltpu.VMEM((tile, tile), bf),
            pltpu.VMEM((COLS, tile, tile), bf),
            pltpu.VMEM((ROWS, tile, tile), bf),
            pltpu.VMEM((COLS, tile, tile), bf),
            pltpu.VMEM((ROWS, SLOT_ROWS, width), bf),
            pltpu.VMEM((ROWS, tile, tile), bf),
            pltpu.VMEM((tile, tile), f32),
            pltpu.VMEM((tile, tile), f32),
            pltpu.SemaphoreType.DMA((N_COPIES,)),
            pltpu.SemaphoreType.DMA((N_COPIES,)),
            pltpu.SemaphoreType.DMA((5,)),
        ],
        compiler_params=pltpu.CompilerParams(
            collective_id=0, has_side_effects=True, vmem_limit_bytes=58 << 20
        ),
    )(
        g0_values,
        sigma_values.reshape(slots * width, width),
        g0_pattern,
        sigma_pairs.reshape(slots, 2).T,
        sigma_count,
    )


def solution(mesh):
    placed = (
        P("row", "col"),
        P("row", "col"),
        P("row", "col", None, None),
        P("row", "col", None),
        P("row", "col"),
    )
    return jax.shard_map(
        per_device, mesh=mesh, in_specs=placed, out_specs=P("row", "col"), check_vma=False
    )
```
